32 devices in a mesh: row: 8 (over z, core), col: 4 (over y, x).
Axes of the slice: x: 2, y: 2, z: 4, core: 2. Of those that a mesh axis runs over, the one named last changes fastest.
Arguments:
- base_weight: bfloat16 [16384, 49152], P('row', 'col'), may hold values from -6 to 6
- left_factor: float32 [16384, 256], P('row', 'col'), may hold values from -6 to 6
- right_factor: float32 [256, 49152], P('row', 'col'), may hold values from -0.375 to 0.375
Outputs:
- merged: bfloat16 [16384, 49152], P(None, ('row', 'col'))
The draws below stay inside these ranges and needn't reach their ends.
All inputs are finite; a program needn't handle non-finite values.
Results may differ from the reference program's by a relative error of at most 0.001.
Values may be sent and summed in bfloat16 or wider, within the bound.
A program may use at most 256 MiB of HBM per device.

```python
import jax
import jax.numpy as jnp
from jax import lax

D = 16384
FF = 49152
RANK = 256
N_ROW = 8


def steps_of(stream_key, shape, pieces, least, high):
    loudness = 1.0
    for dim, parts in pieces:
        draws = jax.random.uniform(jax.random.fold_in(jax.random.fold_in(stream_key, 6), dim), (parts,), jnp.float32, least / len(pieces), high / len(pieces))
        loudness = loudness * jnp.repeat(jnp.exp(draws), shape[dim] // parts).reshape((-1,) + (1,) * (len(shape) - 1 - dim))
    return loudness


def centred(key, shape, spread, most, split=(), dtype=jnp.bfloat16):
    result = jax.random.normal(key, shape, jnp.float32) * spread
    if len(split) > 0:
        result = steps_of(key, shape, split, -0.22, 0.18) * result
    return jnp.clip(result, min=-most, max=most).astype(dtype)


def setup_inputs(seed: int = 0) -> dict:
    key_list = jax.random.split(jax.random.key(seed), 4)
    base_weight = centred(key_list[0], (D, FF), 1.0, 6.0, ((0, 8), (1, 4)))
    left_factor = centred(key_list[1], (D, RANK), 1.0, 6.0, ((0, 8), (1, 4)), jnp.float32)
    right_factor = centred(key_list[2], (RANK, FF), RANK ** -0.5, 0.375, ((0, 8), (1, 4)), jnp.float32)
    return {"base_weight": base_weight, "left_factor": left_factor, "right_factor": right_factor}


def reference(base_weight, left_factor, right_factor):
    left_blocks = left_factor.reshape(N_ROW, D // N_ROW, RANK)
    base_blocks = base_weight.reshape(N_ROW, D // N_ROW, FF)

    def merge_block(pair):
        left_block, base_block = pair
        delta = jnp.dot(left_block, right_factor, precision=lax.Precision.HIGHEST, preferred_element_type=jnp.float32)
        return (base_block.astype(jnp.float32) + delta).astype(jnp.bfloat16)

    merged = lax.map(merge_block, (left_blocks, base_blocks))
    return merged.reshape(D, FF)
```

```python
import functools

import jax
import jax.numpy as jnp
from jax import lax
from jax.experimental import pallas as pl
from jax.experimental.pallas import tpu as pltpu
from jax.sharding import PartitionSpec as P

PARTS = 16
CHUNKS = 15
AHEAD = 3
DELAY = 11
MESH = pl.DeviceIdType.MESH


def transport(nr, nc, base, left, right, served, left_all, right_all, tail, mid, mid_right, *sems):
    (a_send, a_recv, b_send, b_recv, ra_send, ra_recv, rb_send, rb_recv,
     l1_send, l1_recv, l2_send, l2_recv, l3_send, l3_recv, t_send, t_recv, own_sem) = sems
    ng = nr // nc
    planes = nr // 2
    near = planes // 2
    height = base.shape[0]
    width = base.shape[1] // nr
    depth = right.shape[0]
    rank, left_width = left.shape
    step = height // PARTS
    late_rows = height - CHUNKS * step
    r = lax.axis_index("row")
    c = lax.axis_index("col")
    sibling = r + 1 - 2 * lax.rem(r, 2)

    def remote(src, dst, send, recv, row, col):
        return pltpu.make_async_remote_copy(
            src_ref=src, dst_ref=dst, send_sem=send, recv_sem=recv, device_id=(row, col), device_id_type=MESH
        )

    def shifted(value, by, size):
        return lax.rem(value + by + size, size)

    def across(k, dj, g, src, final, middle, rows, send, recv, act):
        j = shifted(c, dj, nc)
        here = c * ng + g == r
        at = pl.ds(pl.multiple_of(k * rows, 8), rows)
        source = src.at[at, pl.ds(pl.multiple_of((g * nc + j) * width, 128), width)]
        sem = (k, dj - 1, g)

        @pl.when(here)
        def _():
            to = final.at[pl.ds(pl.multiple_of(r * src.shape[0] + k * rows, 8), rows), :]
            act(remote(source, to, send.at[sem], recv.at[sem], r, j))

        @pl.when(jnp.logical_not(here))
        def _():
            to = middle.at[c, g, at, :]
            act(remote(source, to, send.at[sem], recv.at[sem], r, j))

    def start(copy):
        copy.start()

    def wait_send(copy):
        copy.wait_send()

    def arrived(k, ds, g, src, final, middle, rows, send, recv):
        at = pl.ds(pl.multiple_of(k * rows, 8), rows)
        s = shifted(c, -ds, nc)
        here = s * ng + g == r
        sem = (k, ds - 1, g)

        @pl.when(here)
        def _():
            to = final.at[pl.ds(pl.multiple_of(r * src.shape[0] + k * rows, 8), rows), :]
            remote(to, to, send.at[sem], recv.at[sem], r, s).wait_recv()

        @pl.when(jnp.logical_not(here))
        def _():
            to = middle.at[s, g, at, :]
            remote(to, to, send.at[sem], recv.at[sem], r, s).wait_recv()

    def along(k, ds, g, src, final, middle, rows, send, recv, own, act, act_own):
        at = pl.ds(pl.multiple_of(k * rows, 8), rows)
        s = shifted(c, -ds, nc)
        to_row = s * ng + g
        if ds == 0:
            source = src.at[at, pl.ds(pl.multiple_of((g * nc + c) * width, 128), width)]
        else:
            source = middle.at[s, g, at, :]
        to = final.at[pl.ds(pl.multiple_of(r * src.shape[0] + k * rows, 8), rows), :]

        @pl.when(to_row != r)
        def _():
            act(remote(source, to, send.at[k, ds, g], recv.at[k, r], to_row, c))

        if ds == 0:
            @pl.when(to_row == r)
            def _():
                act_own(pltpu.make_async_copy(source, to, own.at[k]))

    def received(k, dq, final, rows, total, send, recv):
        q = shifted(r, -dq, nr)
        to = final.at[pl.ds(pl.multiple_of(q * total + k * rows, 8), rows), :]
        remote(to, to, send.at[k, 0, 0], recv.at[k, q], q, c).wait_recv()

    big = (base, served, mid, step)
    small = (right, right_all, mid_right, depth)
    own_big = own_sem.at[pl.ds(0, CHUNKS)]
    own_small = own_sem.at[pl.ds(CHUNKS, 1)]

    def each_across(k, arrays, send, recv, act):
        for dj in range(1, nc):
            for g in range(ng):
                across(k, dj, g, *arrays, send, recv, act)

    def each_along(k, shifts, arrays, send, recv, own, act, act_own):
        for ds in shifts:
            for g in range(ng):
                along(k, ds, g, *arrays, send, recv, own, act, act_own)

    def late_across(dj, g, act):
        j = shifted(c, dj, nc)
        source = base.at[pl.ds(CHUNKS * step, late_rows), pl.ds(pl.multiple_of((g * nc + j) * width, 128), width)]
        act(remote(source, tail.at[c * ng + g], t_send.at[dj - 1, g], t_recv.at[dj - 1, g], r, j))

    def late_arrived(ds, g):
        s = shifted(c, -ds, nc)
        to = tail.at[s * ng + g]
        remote(to, to, t_send.at[ds - 1, g], t_recv.at[ds - 1, g], r, s).wait_recv()

    def late_own(g):
        source = base.at[pl.ds(CHUNKS * step, late_rows), pl.ds(pl.multiple_of((g * nc + c) * width, 128), width)]
        return pltpu.make_async_copy(source, tail.at[c * ng + g], own_sem.at[CHUNKS + 2 + g])

    def each_late(act):
        for dj in range(1, nc):
            for g in range(ng):
                late_across(dj, g, act)

    def block(s, q):
        return left_all.at[
            pl.ds(pl.multiple_of(s * rank, 8), rank), pl.ds(pl.multiple_of(q * left_width, 128), left_width)
        ]

    place = r // 2
    core = lax.rem(r, 2)
    first = place // near * near

    def beside(e):
        return first + lax.rem(place - first + e + near, near)

    def over(p):
        return shifted(p, near, planes)

    def held(m):
        p = beside(-(m % near))
        return (p if m < near else over(p)) * 2 + core

    def first_left(m):
        to = beside(m) if m < near else over(place)
        return remote(left, block(c, r), l1_send.at[m - 1], l1_recv.at[m - 1], to * 2 + core, c)

    def passed_left(m):
        q = held(near)
        return remote(block(c, q), block(c, q), l1_send.at[near + m - 1], l1_recv.at[near + m - 1], beside(m) * 2 + core, c)

    def second_left(d, dj):
        q = held(d)
        source = left if d == 0 else block(c, q)
        return remote(source, block(c, q), l2_send.at[d, dj - 1], l2_recv.at[d, dj - 1], r, shifted(c, dj, nc))

    def third_left(d, ds):
        q = held(d)
        s = shifted(c, -ds, nc)
        source = left if d == 0 and ds == 0 else block(s, q)
        return remote(source, block(s, q), l3_send.at[d, ds], l3_recv.at[d, ds], sibling, c)

    def got(sems_send, sems_recv, s, q):
        remote(block(s, q), block(s, q), sems_send, sems_recv, r, shifted(c, 1, nc)).wait_recv()

    def pass_left():
        got(l1_send.at[near - 1], l1_recv.at[near - 1], c, held(near))
        for m in range(1, near):
            passed_left(m).start()

    def spread_left():
        for d in range(planes):
            if d > 0 and d != near:
                got(l1_send.at[d - 1], l1_recv.at[d - 1], c, held(d))
            for dj in range(1, nc):
                second_left(d, dj).start()
            third_left(d, 0).start()

    def share_left():
        for d in range(planes):
            for ds in range(1, nc):
                got(l2_send.at[d, ds - 1], l2_recv.at[d, ds - 1], shifted(c, -ds, nc), held(d))
                third_left(d, ds).start()

    barrier = pltpu.get_barrier_semaphore()
    for dj in range(1, nc):
        pl.semaphore_signal(barrier, inc=1, device_id=(r, shifted(c, dj, nc)), device_id_type=MESH)
    for dq in range(1, nr):
        pl.semaphore_signal(barrier, inc=1, device_id=(shifted(r, dq, nr), c), device_id_type=MESH)
    pl.semaphore_wait(barrier, nc + nr - 2)

    each_across(0, big, a_send, a_recv, start)
    for m in range(near, 0, -1):
        first_left(m).start()
    each_across(0, small, ra_send, ra_recv, start)
    each_along(0, (0,), small, rb_send, rb_recv, own_small, start, start)
    own_left = pltpu.make_async_copy(left, block(c, r), own_sem.at[CHUNKS + 1])
    own_left.start()

    @pl.loop(1, AHEAD)
    def _(k):
        each_across(k, big, a_send, a_recv, start)

    plane = r // ng
    at_end = jnp.logical_or(r < ng, r >= nr - ng)

    def forward(k):
        for ds in range(nc):
            s = shifted(c, -ds, nc)
            late = jnp.logical_and(at_end, jnp.abs(s - plane) >= 2)
            turn = jnp.where(late, k - DELAY, k)

            @pl.when(jnp.logical_and(turn >= 0, turn < CHUNKS))
            def _():
                for g in range(ng):
                    if ds > 0:
                        arrived(turn, ds, g, *big, a_send, a_recv)
                    along(turn, ds, g, *big, b_send, b_recv, own_big, start, start)

    @pl.loop(0, CHUNKS + DELAY)
    def _(k):
        @pl.when(k + AHEAD < CHUNKS)
        def _():
            each_across(k + AHEAD, big, a_send, a_recv, start)

        @pl.when(k + AHEAD == CHUNKS)
        def _():
            each_late(start)
            for g in range(ng):
                late_own(g).start()

        forward(k)

        for at, act in ((1, pass_left), (5, spread_left), (9, share_left)):
            pl.when(k == at)(act)

        @pl.when(k == 0)
        def _():
            for g in range(ng):
                for ds in range(1, nc):
                    arrived(0, ds, g, *small, ra_send, ra_recv)
            each_along(0, range(1, nc), small, rb_send, rb_recv, own_small, start, start)

    for d in range(planes):
        for ds in range(nc):
            got(l3_send.at[d, ds], l3_recv.at[d, ds], shifted(c, -ds, nc), held(d) + sibling - r)
            third_left(d, ds).wait_send()
        for dj in range(1, nc):
            second_left(d, dj).wait_send()
    for m in range(1, near + 1):
        first_left(m).wait_send()
    for m in range(1, near):
        passed_left(m).wait_send()
    own_left.wait()

    def finish(copy):
        copy.wait()

    def drain(k, arrays, a, b_s, b_r, own):
        each_across(k, arrays, *a, wait_send)
        each_along(k, range(nc), arrays, b_s, b_r, own, wait_send, finish)
        for dq in range(1, nr):
            received(k, dq, arrays[1], arrays[3], arrays[0].shape[0], b_s, b_r)

    each_late(wait_send)
    for g in range(ng):
        late_own(g).wait()
        for ds in range(1, nc):
            late_arrived(ds, g)
    drain(0, small, (ra_send, ra_recv), rb_send, rb_recv, own_small)

    @pl.loop(0, CHUNKS)
    def _(k):
        drain(k, big, (a_send, a_recv), b_send, b_recv, own_big)


def move(base_weight, left_turned, right_factor):
    nr = lax.axis_size("row")
    nc = lax.axis_size("col")
    ng = nr // nc
    planes = nr // 2
    height, stored_width = base_weight.shape
    width = stored_width // nr
    depth = right_factor.shape[0]
    rank, left_width = left_turned.shape
    main_rows = height // PARTS * CHUNKS
    late_rows = height - main_rows
    out = jax.ShapeDtypeStruct
    dma = pltpu.SemaphoreType.DMA
    anywhere = pl.BlockSpec(memory_space=pl.ANY)

    def stage_sems(chunks):
        a = (chunks, nc - 1, ng)
        return [dma(a), dma(a), dma((chunks, nc, ng)), dma((chunks, nr))]

    return pl.pallas_call(
        functools.partial(transport, nr, nc),
        out_shape=[
            out((nr * height, width), base_weight.dtype),
            out((nc * rank, nr * left_width), left_turned.dtype),
            out((nr * depth, width), right_factor.dtype),
            out((nr, late_rows, width), base_weight.dtype),
            out((nc, ng, main_rows, width), base_weight.dtype),
            out((nc, ng, depth, width), right_factor.dtype),
        ],
        in_specs=[anywhere] * 3,
        out_specs=[anywhere] * 6,
        scratch_shapes=[
            *stage_sems(CHUNKS),
            *stage_sems(1),
            dma((planes - 1,)), dma((planes - 1,)),
            dma((planes, nc - 1)), dma((planes, nc - 1)),
            dma((planes, nc)), dma((planes, nc)),
            dma((nc - 1, ng)), dma((nc - 1, ng)),
            dma((CHUNKS + 2 + ng,)),
        ],
        compiler_params=pltpu.CompilerParams(collective_id=0, has_side_effects=True),
    )(base_weight, left_turned, right_factor)


def product(left, right):
    return lax.dot_general(
        left, right, (((0,), (0,)), ((), ())), precision=lax.Precision.HIGH, preferred_element_type=jnp.float32
    )


def body(base_weight, left_factor, right_factor):
    nr = lax.axis_size("row")
    height = base_weight.shape[0]
    served, left_all, right_all, tail, _, _ = move(base_weight, left_factor.T, right_factor)
    late = lax.all_to_all(tail, "row", 0, 0)
    late_rows, width = late.shape[1:]
    merged = (served.astype(jnp.float32) + product(left_all, right_all)).astype(jnp.bfloat16)
    late_left = jnp.concatenate([left_all[:, (q + 1) * height - late_rows:(q + 1) * height] for q in range(nr)], axis=1)
    late_merged = late.astype(jnp.float32) + product(late_left, right_all).reshape(late.shape)
    merged = merged.reshape(nr, height, width).at[:, height - late_rows:].set(late_merged.astype(jnp.bfloat16))
    return merged.reshape(nr * height, width)


def solution(mesh):
    placed = (P("row", "col"), P("row", "col"), P("row", "col"))
    return jax.shard_map(
        body, mesh=mesh, in_specs=placed, out_specs=P(None, ("row", "col")), check_vma=False
    )
```

```python
import functools

import jax
import jax.numpy as jnp
from jax import lax
from jax.experimental import pallas as pl
from jax.experimental.pallas import tpu as pltpu
from jax.sharding import PartitionSpec as P

PARTS = 16
CHUNKS = 15
AHEAD = 4
MESH = pl.DeviceIdType.MESH


def transport(nr, nc, base, left, right, served, left_all, right_all, tail, mid, mid_right, *sems):
    (a_send, a_recv, b_send, b_recv, ra_send, ra_recv, rb_send, rb_recv,
     l1_send, l1_recv, l2_send, l2_recv, l3_send, l3_recv, t_send, t_recv, own_sem) = sems
    ng = nr // nc
    planes = nr // 2
    near = planes // 2
    height = base.shape[0]
    width = base.shape[1] // nr
    depth = right.shape[0]
    rank, left_width = left.shape
    step = height // PARTS
    late_rows = height - CHUNKS * step
    r = lax.axis_index("row")
    c = lax.axis_index("col")
    sibling = r + 1 - 2 * lax.rem(r, 2)

    def remote(src, dst, send, recv, row, col):
        return pltpu.make_async_remote_copy(
            src_ref=src, dst_ref=dst, send_sem=send, recv_sem=recv, device_id=(row, col), device_id_type=MESH
        )

    def shifted(value, by, size):
        return lax.rem(value + by + size, size)

    def across(k, dj, g, src, final, middle, rows, send, recv, act):
        j = shifted(c, dj, nc)
        here = c * ng + g == r
        at = pl.ds(pl.multiple_of(k * rows, 8), rows)
        source = src.at[at, pl.ds(pl.multiple_of((g * nc + j) * width, 128), width)]
        sem = (k, dj - 1, g)

        @pl.when(here)
        def _():
            to = final.at[pl.ds(pl.multiple_of(r * src.shape[0] + k * rows, 8), rows), :]
            act(remote(source, to, send.at[sem], recv.at[sem], r, j))

        @pl.when(jnp.logical_not(here))
        def _():
            to = middle.at[c, g, at, :]
            act(remote(source, to, send.at[sem], recv.at[sem], r, j))

    def start(copy):
        copy.start()

    def wait_send(copy):
        copy.wait_send()

    def arrived(k, ds, g, src, final, middle, rows, send, recv):
        at = pl.ds(pl.multiple_of(k * rows, 8), rows)
        s = shifted(c, -ds, nc)
        here = s * ng + g == r
        sem = (k, ds - 1, g)

        @pl.when(here)
        def _():
            to = final.at[pl.ds(pl.multiple_of(r * src.shape[0] + k * rows, 8), rows), :]
            remote(to, to, send.at[sem], recv.at[sem], r, s).wait_recv()

        @pl.when(jnp.logical_not(here))
        def _():
            to = middle.at[s, g, at, :]
            remote(to, to, send.at[sem], recv.at[sem], r, s).wait_recv()

    def along(k, ds, g, src, final, middle, rows, send, recv, own, act, act_own):
        at = pl.ds(pl.multiple_of(k * rows, 8), rows)
        s = shifted(c, -ds, nc)
        to_row = s * ng + g
        if ds == 0:
            source = src.at[at, pl.ds(pl.multiple_of((g * nc + c) * width, 128), width)]
        else:
            source = middle.at[s, g, at, :]
        to = final.at[pl.ds(pl.multiple_of(r * src.shape[0] + k * rows, 8), rows), :]

        @pl.when(to_row != r)
        def _():
            act(remote(source, to, send.at[k, ds, g], recv.at[k, r], to_row, c))

        if ds == 0:
            @pl.when(to_row == r)
            def _():
                act_own(pltpu.make_async_copy(source, to, own.at[k]))

    def received(k, dq, final, rows, total, send, recv):
        q = shifted(r, -dq, nr)
        to = final.at[pl.ds(pl.multiple_of(q * total + k * rows, 8), rows), :]
        remote(to, to, send.at[k, 0, 0], recv.at[k, q], q, c).wait_recv()

    big = (base, served, mid, step)
    small = (right, right_all, mid_right, depth)
    own_big = own_sem.at[pl.ds(0, CHUNKS)]
    own_small = own_sem.at[pl.ds(CHUNKS, 1)]

    def each_across(k, arrays, send, recv, act):
        for dj in range(1, nc):
            for g in range(ng):
                across(k, dj, g, *arrays, send, recv, act)

    def each_along(k, shifts, arrays, send, recv, own, act, act_own):
        for ds in shifts:
            for g in range(ng):
                along(k, ds, g, *arrays, send, recv, own, act, act_own)

    def late_across(dj, g, act):
        j = shifted(c, dj, nc)
        source = base.at[pl.ds(CHUNKS * step, late_rows), pl.ds(pl.multiple_of((g * nc + j) * width, 128), width)]
        act(remote(source, tail.at[c * ng + g], t_send.at[dj - 1, g], t_recv.at[dj - 1, g], r, j))

    def late_arrived(ds, g):
        s = shifted(c, -ds, nc)
        to = tail.at[s * ng + g]
        remote(to, to, t_send.at[ds - 1, g], t_recv.at[ds - 1, g], r, s).wait_recv()

    def late_own(g):
        source = base.at[pl.ds(CHUNKS * step, late_rows), pl.ds(pl.multiple_of((g * nc + c) * width, 128), width)]
        return pltpu.make_async_copy(source, tail.at[c * ng + g], own_sem.at[CHUNKS + 2 + g])

    def each_late(act):
        for dj in range(1, nc):
            for g in range(ng):
                late_across(dj, g, act)

    def block(s, q):
        return left_all.at[
            pl.ds(pl.multiple_of(s * rank, 8), rank), pl.ds(pl.multiple_of(q * left_width, 128), left_width)
        ]

    place = r // 2
    core = lax.rem(r, 2)
    first = place // near * near

    def beside(e):
        return first + lax.rem(place - first + e + near, near)

    def over(p):
        return shifted(p, near, planes)

    def held(m):
        p = beside(-(m % near))
        return (p if m < near else over(p)) * 2 + core

    def first_left(m):
        to = beside(m) if m < near else over(place)
        return remote(left, block(c, r), l1_send.at[m - 1], l1_recv.at[m - 1], to * 2 + core, c)

    def passed_left(m):
        q = held(near)
        return remote(block(c, q), block(c, q), l1_send.at[near + m - 1], l1_recv.at[near + m - 1], beside(m) * 2 + core, c)

    def second_left(d, dj):
        q = held(d)
        source = left if d == 0 else block(c, q)
        return remote(source, block(c, q), l2_send.at[d, dj - 1], l2_recv.at[d, dj - 1], r, shifted(c, dj, nc))

    def third_left(d, ds):
        q = held(d)
        s = shifted(c, -ds, nc)
        source = left if d == 0 and ds == 0 else block(s, q)
        return remote(source, block(s, q), l3_send.at[d, ds], l3_recv.at[d, ds], sibling, c)

    def got(sems_send, sems_recv, s, q):
        remote(block(s, q), block(s, q), sems_send, sems_recv, r, shifted(c, 1, nc)).wait_recv()

    def pass_left():
        got(l1_send.at[near - 1], l1_recv.at[near - 1], c, held(near))
        for m in range(1, near):
            passed_left(m).start()

    def spread_left():
        for d in range(planes):
            if d > 0 and d != near:
                got(l1_send.at[d - 1], l1_recv.at[d - 1], c, held(d))
            for dj in range(1, nc):
                second_left(d, dj).start()
            third_left(d, 0).start()

    def share_left():
        for d in range(planes):
            for ds in range(1, nc):
                got(l2_send.at[d, ds - 1], l2_recv.at[d, ds - 1], shifted(c, -ds, nc), held(d))
                third_left(d, ds).start()

    barrier = pltpu.get_barrier_semaphore()
    for dj in range(1, nc):
        pl.semaphore_signal(barrier, inc=1, device_id=(r, shifted(c, dj, nc)), device_id_type=MESH)
    for dq in range(1, nr):
        pl.semaphore_signal(barrier, inc=1, device_id=(shifted(r, dq, nr), c), device_id_type=MESH)
    pl.semaphore_wait(barrier, nc + nr - 2)

    each_across(0, big, a_send, a_recv, start)
    for m in range(near, 0, -1):
        first_left(m).start()
    each_across(0, small, ra_send, ra_recv, start)
    each_along(0, (0,), small, rb_send, rb_recv, own_small, start, start)
    own_left = pltpu.make_async_copy(left, block(c, r), own_sem.at[CHUNKS + 1])
    own_left.start()

    @pl.loop(1, AHEAD)
    def _(k):
        each_across(k, big, a_send, a_recv, start)

    def forward(k):
        for ds in range(nc):
            for g in range(ng):
                if ds > 0:
                    arrived(k, ds, g, *big, a_send, a_recv)
                along(k, ds, g, *big, b_send, b_recv, own_big, start, start)

    @pl.loop(0, CHUNKS)
    def _(k):
        @pl.when(k + AHEAD < CHUNKS)
        def _():
            each_across(k + AHEAD, big, a_send, a_recv, start)

        @pl.when(k + AHEAD == CHUNKS)
        def _():
            each_late(start)
            for g in range(ng):
                late_own(g).start()

        forward(k)

        for at, act in ((1, pass_left), (5, spread_left), (9, share_left)):
            pl.when(k == at)(act)

        @pl.when(k == 0)
        def _():
            for g in range(ng):
                for ds in range(1, nc):
                    arrived(0, ds, g, *small, ra_send, ra_recv)
            each_along(0, range(1, nc), small, rb_send, rb_recv, own_small, start, start)

    for d in range(planes):
        for ds in range(nc):
            got(l3_send.at[d, ds], l3_recv.at[d, ds], shifted(c, -ds, nc), held(d) + sibling - r)
            third_left(d, ds).wait_send()
        for dj in range(1, nc):
            second_left(d, dj).wait_send()
    for m in range(1, near + 1):
        first_left(m).wait_send()
    for m in range(1, near):
        passed_left(m).wait_send()
    own_left.wait()

    def finish(copy):
        copy.wait()

    def drain(k, arrays, a, b_s, b_r, own):
        each_across(k, arrays, *a, wait_send)
        each_along(k, range(nc), arrays, b_s, b_r, own, wait_send, finish)
        for dq in range(1, nr):
            received(k, dq, arrays[1], arrays[3], arrays[0].shape[0], b_s, b_r)

    each_late(wait_send)
    for g in range(ng):
        late_own(g).wait()
        for ds in range(1, nc):
            late_arrived(ds, g)
    drain(0, small, (ra_send, ra_recv), rb_send, rb_recv, own_small)

    @pl.loop(0, CHUNKS)
    def _(k):
        drain(k, big, (a_send, a_recv), b_send, b_recv, own_big)


def move(base_weight, left_turned, right_factor):
    nr = lax.axis_size("row")
    nc = lax.axis_size("col")
    ng = nr // nc
    planes = nr // 2
    height, stored_width = base_weight.shape
    width = stored_width // nr
    depth = right_factor.shape[0]
    rank, left_width = left_turned.shape
    main_rows = height // PARTS * CHUNKS
    late_rows = height - main_rows
    out = jax.ShapeDtypeStruct
    dma = pltpu.SemaphoreType.DMA
    anywhere = pl.BlockSpec(memory_space=pl.ANY)

    def stage_sems(chunks):
        a = (chunks, nc - 1, ng)
        return [dma(a), dma(a), dma((chunks, nc, ng)), dma((chunks, nr))]

    return pl.pallas_call(
        functools.partial(transport, nr, nc),
        out_shape=[
            out((nr * height, width), base_weight.dtype),
            out((nc * rank, nr * left_width), left_turned.dtype),
            out((nr * depth, width), right_factor.dtype),
            out((nr, late_rows, width), base_weight.dtype),
            out((nc, ng, main_rows, width), base_weight.dtype),
            out((nc, ng, depth, width), right_factor.dtype),
        ],
        in_specs=[anywhere] * 3,
        out_specs=[anywhere] * 6,
        scratch_shapes=[
            *stage_sems(CHUNKS),
            *stage_sems(1),
            dma((planes - 1,)), dma((planes - 1,)),
            dma((planes, nc - 1)), dma((planes, nc - 1)),
            dma((planes, nc)), dma((planes, nc)),
            dma((nc - 1, ng)), dma((nc - 1, ng)),
            dma((CHUNKS + 2 + ng,)),
        ],
        compiler_params=pltpu.CompilerParams(collective_id=0, has_side_effects=True),
    )(base_weight, left_turned, right_factor)


def product(left, right):
    return lax.dot_general(
        left, right, (((0,), (0,)), ((), ())), precision=lax.Precision.HIGH, preferred_element_type=jnp.float32
    )


def body(base_weight, left_factor, right_factor):
    nr = lax.axis_size("row")
    height = base_weight.shape[0]
    served, left_all, right_all, tail, _, _ = move(base_weight, left_factor.T, right_factor)
    late = lax.all_to_all(tail, "row", 0, 0)
    late_rows, width = late.shape[1:]
    merged = (served.astype(jnp.float32) + product(left_all, right_all)).astype(jnp.bfloat16)
    late_left = jnp.concatenate([left_all[:, (q + 1) * height - late_rows:(q + 1) * height] for q in range(nr)], axis=1)
    late_merged = late.astype(jnp.float32) + product(late_left, right_all).reshape(late.shape)
    merged = merged.reshape(nr, height, width).at[:, height - late_rows:].set(late_merged.astype(jnp.bfloat16))
    return merged.reshape(nr * height, width)


def solution(mesh):
    placed = (P("row", "col"), P("row", "col"), P("row", "col"))
    return jax.shard_map(
        body, mesh=mesh, in_specs=placed, out_specs=P(None, ("row", "col")), check_vma=False
    )
```

```python
import functools

import jax
import jax.numpy as jnp
from jax import lax
from jax.experimental import pallas as pl
from jax.experimental.pallas import tpu as pltpu
from jax.sharding import PartitionSpec as P

PARTS = 16
CHUNKS = 15
FINE = 8
AHEAD = 4
CODE_AT = 1
PASS_AT = 3
SMALL_AT = 6
SPREAD_AT = 7
SHARE_AT = 13
MESH = pl.DeviceIdType.MESH
LANES = 128
GROUP = 16
OCTAVES = 251
LOWEST = -125.0
LEVELS = OCTAVES * 128.0 - 1.0


def coded(value):
    top = jnp.max(jnp.abs(value), axis=1, keepdims=True)
    scale = jnp.maximum(top * 1.01, 1e-30).astype(jnp.bfloat16)
    level = jnp.floor(jnp.abs(value) * (LEVELS / scale.astype(jnp.float32)) + 0.5)
    octave = jnp.floor(level * (1.0 / 128.0))
    word = (level * (1.0 / 128.0) - octave + 1.0) * jnp.exp2(octave + LOWEST)
    return jnp.where(value < 0.0, -word, word).astype(jnp.bfloat16), scale


def decoded(word, scale):
    word = word.astype(jnp.float32)
    size = jnp.abs(word)
    octave = jnp.floor(jnp.log2(size))
    level = jnp.floor((octave - LOWEST + (size * jnp.exp2(-octave) - 1.0)) * 128.0 + 0.5)
    value = level * (scale.astype(jnp.float32) * (1.0 / LEVELS))
    return jnp.where(word < 0.0, -value, value)


def encode_rows(source, target, width):
    @pl.loop(0, source.shape[0] // GROUP)
    def _(i):
        rows = pl.ds(pl.multiple_of(i * GROUP, GROUP), GROUP)
        for b in range(source.shape[1] // width):
            word, scale = coded(source[rows, b * width:(b + 1) * width])
            target[b, rows, :width] = word
            target[b, rows, width:] = jnp.broadcast_to(scale, (GROUP, LANES))


def decode_rows(source, target):
    width = target.shape[1]

    @pl.loop(0, source.shape[0] // GROUP)
    def _(i):
        rows = pl.ds(pl.multiple_of(i * GROUP, GROUP), GROUP)
        target[rows, :] = decoded(source[rows, :width], source[rows, width:width + 1])


def transport(
    nr, nc, base, left, right, served, left_all, right_all, tail, mid, mid_right,
    left_code, left_codes, right_code, right_codes, *scratch,
):
    (a_send, a_recv, b_send, b_recv, fa_send, fa_recv, fb_send, fb_recv, ra_send, ra_recv, rb_send, rb_recv,
     l1_send, l1_recv, l2_send, l2_recv, l3_send, l3_recv, t_send, t_recv, own_sem, code_sem,
     left_in, left_out, right_in, right_out, left_words, left_values, right_words, right_values) = scratch
    ng = nr // nc
    planes = nr // 2
    near = planes // 2
    height = base.shape[0]
    width = base.shape[1] // nr
    depth = right.shape[0]
    rank = left.shape[0]
    left_width = left_code.shape[2]
    step = height // PARTS
    late_rows = height - CHUNKS * step
    r = lax.axis_index("row")
    c = lax.axis_index("col")
    sibling = r + 1 - 2 * lax.rem(r, 2)

    def remote(src, dst, send, recv, row, col):
        return pltpu.make_async_remote_copy(
            src_ref=src, dst_ref=dst, send_sem=send, recv_sem=recv, device_id=(row, col), device_id_type=MESH
        )

    def shifted(value, by, size):
        return lax.rem(value + by + size, size)

    def piece(src, at, b):
        if len(src.shape) == 3:
            return src.at[b]
        return src.at[at, pl.ds(pl.multiple_of(b * width, 128), width)]

    def tall(src):
        return src.shape[-2]

    def across(k, dj, g, src, final, middle, rows, send, recv, act):
        j = shifted(c, dj, nc)
        here = c * ng + g == r
        at = pl.ds(pl.multiple_of(k * rows, 8), rows)
        source = piece(src, at, g * nc + j)
        sem = (k, dj - 1, g)

        @pl.when(here)
        def _():
            to = final.at[pl.ds(pl.multiple_of(r * tall(src) + k * rows, 8), rows), :]
            act(remote(source, to, send.at[sem], recv.at[sem], r, j))

        @pl.when(jnp.logical_not(here))
        def _():
            to = middle.at[c, g, at, :]
            act(remote(source, to, send.at[sem], recv.at[sem], r, j))

    def start(copy):
        copy.start()

    def wait_send(copy):
        copy.wait_send()

    def arrived(k, ds, g, src, final, middle, rows, send, recv):
        at = pl.ds(pl.multiple_of(k * rows, 8), rows)
        s = shifted(c, -ds, nc)
        here = s * ng + g == r
        sem = (k, ds - 1, g)

        @pl.when(here)
        def _():
            to = final.at[pl.ds(pl.multiple_of(r * tall(src) + k * rows, 8), rows), :]
            remote(to, to, send.at[sem], recv.at[sem], r, s).wait_recv()

        @pl.when(jnp.logical_not(here))
        def _():
            to = middle.at[s, g, at, :]
            remote(to, to, send.at[sem], recv.at[sem], r, s).wait_recv()

    def along(k, ds, g, src, final, middle, rows, send, recv, own, act, act_own):
        at = pl.ds(pl.multiple_of(k * rows, 8), rows)
        s = shifted(c, -ds, nc)
        to_row = s * ng + g
        if ds == 0:
            source = piece(src, at, g * nc + c)
        else:
            source = middle.at[s, g, at, :]
        to = final.at[pl.ds(pl.multiple_of(r * tall(src) + k * rows, 8), rows), :]

        @pl.when(to_row != r)
        def _():
            act(remote(source, to, send.at[k, ds, g], recv.at[k, r], to_row, c))

        if ds == 0:
            @pl.when(to_row == r)
            def _():
                act_own(pltpu.make_async_copy(source, to, own.at[k]))

    def received(k, dq, final, rows, total, send, recv):
        q = shifted(r, -dq, nr)
        to = final.at[pl.ds(pl.multiple_of(q * total + k * rows, 8), rows), :]
        remote(to, to, send.at[k, 0, 0], recv.at[k, q], q, c).wait_recv()

    big = (base, served, mid, step)
    fine = (base, served, mid, step // FINE)
    small = (right_code, right_codes, mid_right, depth)
    order = (nc // 2, *(d for d in range(1, nc) if d != nc // 2))
    own_big = own_sem.at[pl.ds(0, CHUNKS)]
    own_small = own_sem.at[pl.ds(CHUNKS, 1)]
    own_fine = own_sem.at[pl.ds(CHUNKS + 2 + ng, FINE)]

    def each_across(k, arrays, send, recv, act):
        for dj in order:
            for g in range(ng):
                across(k, dj, g, *arrays, send, recv, act)

    def each_along(k, shifts, arrays, send, recv, own, act, act_own):
        for ds in shifts:
            for g in range(ng):
                along(k, ds, g, *arrays, send, recv, own, act, act_own)

    def late_across(dj, g, act):
        j = shifted(c, dj, nc)
        source = base.at[pl.ds(CHUNKS * step, late_rows), pl.ds(pl.multiple_of((g * nc + j) * width, 128), width)]
        act(remote(source, tail.at[c * ng + g], t_send.at[dj - 1, g], t_recv.at[dj - 1, g], r, j))

    def late_arrived(ds, g):
        s = shifted(c, -ds, nc)
        to = tail.at[s * ng + g]
        remote(to, to, t_send.at[ds - 1, g], t_recv.at[ds - 1, g], r, s).wait_recv()

    def late_own(g):
        source = base.at[pl.ds(CHUNKS * step, late_rows), pl.ds(pl.multiple_of((g * nc + c) * width, 128), width)]
        return pltpu.make_async_copy(source, tail.at[c * ng + g], own_sem.at[CHUNKS + 2 + g])

    def each_late(act):
        for dj in range(1, nc):
            for g in range(ng):
                late_across(dj, g, act)

    def block(s, q):
        return left_codes.at[
            pl.ds(pl.multiple_of(s * rank, 8), rank), pl.ds(pl.multiple_of(q * left_width, 128), left_width)
        ]

    place = r // 2
    core = lax.rem(r, 2)
    first = place // near * near

    def beside(e):
        return first + lax.rem(place - first + e + near, near)

    def over(p):
        return shifted(p, near, planes)

    def held(m):
        p = beside(-(m % near))
        return (p if m < near else over(p)) * 2 + core

    def first_left(m):
        to = beside(m) if m < near else over(place)
        return remote(left_code.at[0], block(c, r), l1_send.at[m - 1], l1_recv.at[m - 1], to * 2 + core, c)

    def passed_left(m):
        q = held(near)
        return remote(block(c, q), block(c, q), l1_send.at[near + m - 1], l1_recv.at[near + m - 1], beside(m) * 2 + core, c)

    def second_left(d, dj):
        q = held(d)
        source = left_code.at[0] if d == 0 else block(c, q)
        return remote(source, block(c, q), l2_send.at[d, dj - 1], l2_recv.at[d, dj - 1], r, shifted(c, dj, nc))

    def third_left(d, ds):
        q = held(d)
        s = shifted(c, -ds, nc)
        source = left_code.at[0] if d == 0 and ds == 0 else block(s, q)
        return remote(source, block(s, q), l3_send.at[d, ds], l3_recv.at[d, ds], sibling, c)

    def got(sems_send, sems_recv, s, q):
        remote(block(s, q), block(s, q), sems_send, sems_recv, r, shifted(c, 1, nc)).wait_recv()

    def pass_left():
        got(l1_send.at[near - 1], l1_recv.at[near - 1], c, held(near))
        for m in range(1, near):
            passed_left(m).start()

    def spread_left():
        for d in range(planes):
            if d > 0 and d != near:
                got(l1_send.at[d - 1], l1_recv.at[d - 1], c, held(d))
            for dj in range(1, nc):
                second_left(d, dj).start()
            third_left(d, 0).start()

    def share_left():
        for d in range(planes):
            for ds in range(1, nc):
                got(l2_send.at[d, ds - 1], l2_recv.at[d, ds - 1], shifted(c, -ds, nc), held(d))
                third_left(d, ds).start()

    barrier = pltpu.get_barrier_semaphore()
    for dj in range(1, nc):
        pl.semaphore_signal(barrier, inc=1, device_id=(r, shifted(c, dj, nc)), device_id_type=MESH)
    for dq in range(1, nr):
        pl.semaphore_signal(barrier, inc=1, device_id=(shifted(r, dq, nr), c), device_id_type=MESH)
    pl.semaphore_wait(barrier, nc + nr - 2)

    fetch_left = pltpu.make_async_copy(left, left_in, code_sem.at[0])
    fetch_right = pltpu.make_async_copy(right, right_in, code_sem.at[1])
    fetch_left.start()
    fetch_right.start()
    for k in range(FINE):
        each_across(k, fine, fa_send, fa_recv, start)
        each_along(k, (0,), fine, fb_send, fb_recv, own_fine, start, start)

    @pl.loop(1, AHEAD + 1)
    def _(k):
        each_across(k, big, a_send, a_recv, start)

    own_left = pltpu.make_async_copy(left_code.at[0], block(c, r), own_sem.at[CHUNKS + 1])

    def send_codes():
        fetch_left.wait()
        encode_rows(left_in, left_out, left.shape[1])
        keep_left = pltpu.make_async_copy(left_out, left_code, code_sem.at[2])
        keep_left.start()
        fetch_right.wait()
        encode_rows(right_in, right_out, width)
        keep_right = pltpu.make_async_copy(right_out, right_code, code_sem.at[3])
        keep_right.start()
        keep_left.wait()
        for m in range(near, 0, -1):
            first_left(m).start()
        own_left.start()
        keep_right.wait()
        each_across(0, small, ra_send, ra_recv, start)
        each_along(0, (0,), small, rb_send, rb_recv, own_small, start, start)

    def forward(k, arrays, a_s, a_r, b_s, b_r, own):
        for ds in order:
            for g in range(ng):
                arrived(k, ds, g, *arrays, a_s, a_r)
                along(k, ds, g, *arrays, b_s, b_r, own, start, start)

    for k in range(FINE):
        forward(k, fine, fa_send, fa_recv, fb_send, fb_recv, own_fine)
    each_along(1, (0,), big, b_send, b_recv, own_big, start, start)

    @pl.loop(1, CHUNKS)
    def _(k):
        @pl.when(k + AHEAD < CHUNKS)
        def _():
            each_across(k + AHEAD, big, a_send, a_recv, start)

        @pl.when(k + AHEAD == CHUNKS)
        def _():
            each_late(start)
            for g in range(ng):
                late_own(g).start()

        forward(k, big, a_send, a_recv, b_send, b_recv, own_big)

        @pl.when(k + 1 < CHUNKS)
        def _():
            each_along(k + 1, (0,), big, b_send, b_recv, own_big, start, start)

        for at, act in ((CODE_AT, send_codes), (PASS_AT, pass_left), (SPREAD_AT, spread_left), (SHARE_AT, share_left)):
            pl.when(k == at)(act)

        @pl.when(k == SMALL_AT)
        def _():
            for g in range(ng):
                for ds in order:
                    arrived(0, ds, g, *small, ra_send, ra_recv)
            each_along(0, range(1, nc), small, rb_send, rb_recv, own_small, start, start)

    for d in range(planes):
        for ds in range(nc):
            got(l3_send.at[d, ds], l3_recv.at[d, ds], shifted(c, -ds, nc), held(d) + sibling - r)
            third_left(d, ds).wait_send()
        for dj in range(1, nc):
            second_left(d, dj).wait_send()
    for m in range(1, near + 1):
        first_left(m).wait_send()
    for m in range(1, near):
        passed_left(m).wait_send()
    own_left.wait()

    def finish(copy):
        copy.wait()

    def drain(k, arrays, a, b_s, b_r, own):
        each_across(k, arrays, *a, wait_send)
        each_along(k, range(nc), arrays, b_s, b_r, own, wait_send, finish)
        for dq in range(1, nr):
            received(k, dq, arrays[1], arrays[3], tall(arrays[0]), b_s, b_r)

    drain(0, small, (ra_send, ra_recv), rb_send, rb_recv, own_small)
    words = pltpu.make_async_copy(right_codes, right_words, code_sem.at[0])
    words.start()
    words.wait()
    decode_rows(right_words, right_values)
    values = pltpu.make_async_copy(right_values, right_all, code_sem.at[1])
    values.start()
    values.wait()

    @pl.loop(0, nr)
    def _(q):
        part = left_codes.at[:, pl.ds(pl.multiple_of(q * left_width, 128), left_width)]
        rows = left.shape[1]
        to = left_all.at[:, pl.ds(pl.multiple_of(q * rows, 128), rows)]
        words = pltpu.make_async_copy(part, left_words, code_sem.at[2])
        words.start()
        words.wait()
        decode_rows(left_words, left_values)
        values = pltpu.make_async_copy(left_values, to, code_sem.at[3])
        values.start()
        values.wait()

    each_late(wait_send)
    for g in range(ng):
        late_own(g).wait()
        for ds in range(1, nc):
            late_arrived(ds, g)
    for k in range(FINE):
        drain(k, fine, (fa_send, fa_recv), fb_send, fb_recv, own_fine)

    @pl.loop(1, CHUNKS)
    def _(k):
        drain(k, big, (a_send, a_recv), b_send, b_recv, own_big)


def move(base_weight, left_turned, right_factor):
    nr = lax.axis_size("row")
    nc = lax.axis_size("col")
    ng = nr // nc
    planes = nr // 2
    height, stored_width = base_weight.shape
    width = stored_width // nr
    depth = right_factor.shape[0]
    rank, left_width = left_turned.shape
    main_rows = height // PARTS * CHUNKS
    late_rows = height - main_rows
    out = jax.ShapeDtypeStruct
    code = jnp.bfloat16
    vmem = pltpu.VMEM
    dma = pltpu.SemaphoreType.DMA
    anywhere = pl.BlockSpec(memory_space=pl.ANY)

    def stage_sems(chunks):
        a = (chunks, nc - 1, ng)
        return [dma(a), dma(a), dma((chunks, nc, ng)), dma((chunks, nr))]

    return pl.pallas_call(
        functools.partial(transport, nr, nc),
        out_shape=[
            out((nr * height, width), base_weight.dtype),
            out((nc * rank, nr * left_width), left_turned.dtype),
            out((nr * depth, width), right_factor.dtype),
            out((nr, late_rows, width), base_weight.dtype),
            out((nc, ng, main_rows, width), base_weight.dtype),
            out((nc, ng, depth, width + LANES), code),
            out((1, rank, left_width + LANES), code),
            out((nc * rank, nr * (left_width + LANES)), code),
            out((nr, depth, width + LANES), code),
            out((nr * depth, width + LANES), code),
        ],
        in_specs=[anywhere] * 3,
        out_specs=[anywhere] * 10,
        scratch_shapes=[
            *stage_sems(CHUNKS),
            *stage_sems(FINE),
            *stage_sems(1),
            dma((planes - 1,)), dma((planes - 1,)),
            dma((planes, nc - 1)), dma((planes, nc - 1)),
            dma((planes, nc)), dma((planes, nc)),
            dma((nc - 1, ng)), dma((nc - 1, ng)),
            dma((CHUNKS + 2 + ng + FINE,)), dma((4,)),
            vmem((rank, left_width), jnp.float32), vmem((1, rank, left_width + LANES), code),
            vmem((depth, stored_width), jnp.float32), vmem((nr, depth, width + LANES), code),
            vmem((nc * rank, left_width + LANES), code), vmem((nc * rank, left_width), jnp.float32),
            vmem((nr * depth, width + LANES), code), vmem((nr * depth, width), jnp.float32),
        ],
        compiler_params=pltpu.CompilerParams(collective_id=0, has_side_effects=True),
    )(base_weight, left_turned, right_factor)


def product(left, right):
    return lax.dot_general(
        left, right, (((0,), (0,)), ((), ())), precision=lax.Precision.HIGH, preferred_element_type=jnp.float32
    )


def body(base_weight, left_factor, right_factor):
    nr = lax.axis_size("row")
    height = base_weight.shape[0]
    served, left_all, right_all, tail, *_ = move(base_weight, left_factor.T, right_factor)
    late = lax.all_to_all(tail, "row", 0, 0)
    late_rows, width = late.shape[1:]
    merged = (served.astype(jnp.float32) + product(left_all, right_all)).astype(jnp.bfloat16)
    late_left = jnp.concatenate([left_all[:, (q + 1) * height - late_rows:(q + 1) * height] for q in range(nr)], axis=1)
    late_merged = late.astype(jnp.float32) + product(late_left, right_all).reshape(late.shape)
    merged = merged.reshape(nr, height, width).at[:, height - late_rows:].set(late_merged.astype(jnp.bfloat16))
    return merged.reshape(nr * height, width)


def solution(mesh):
    placed = (P("row", "col"), P("row", "col"), P("row", "col"))
    return jax.shard_map(
        body, mesh=mesh, in_specs=placed, out_specs=P(None, ("row", "col")), check_vma=False
    )
```

```python
import functools

import jax
import jax.numpy as jnp
from jax import lax
from jax.experimental import pallas as pl
from jax.experimental.pallas import tpu as pltpu
from jax.sharding import PartitionSpec as P

PARTS = 16
CHUNKS = 15
FINE = 8
LATE = 16
LATE_PARTS = 1
AHEAD = 4
CODE_AT = 5
PASS_AT = 4
SMALL_AT = 10
SPREAD_AT = 10
SHARE_AT = 14
MESH = pl.DeviceIdType.MESH
LANES = 128
GROUP = 16
OCTAVES = 251
LOWEST = -125.0
LEVELS = OCTAVES * 128.0 - 1.0


def coded(value):
    top = jnp.max(jnp.abs(value), axis=1, keepdims=True)
    scale = jnp.maximum(top * 1.01, 1e-30).astype(jnp.bfloat16)
    level = jnp.floor(jnp.abs(value) * (LEVELS / scale.astype(jnp.float32)) + 0.5)
    octave = jnp.floor(level * (1.0 / 128.0))
    word = (level * (1.0 / 128.0) - octave + 1.0) * jnp.exp2(octave + LOWEST)
    return jnp.where(value < 0.0, -word, word).astype(jnp.bfloat16), scale


def decoded(word, scale):
    word = word.astype(jnp.float32)
    size = jnp.abs(word)
    octave = jnp.floor(jnp.log2(size))
    level = jnp.floor((octave - LOWEST + (size * jnp.exp2(-octave) - 1.0)) * 128.0 + 0.5)
    value = level * (scale.astype(jnp.float32) * (1.0 / LEVELS))
    return jnp.where(word < 0.0, -value, value)


def encode_rows(source, target, width):
    @pl.loop(0, source.shape[0] // GROUP)
    def _(i):
        rows = pl.ds(pl.multiple_of(i * GROUP, GROUP), GROUP)
        for b in range(source.shape[1] // width):
            word, scale = coded(source[rows, b * width:(b + 1) * width])
            target[b, rows, :width] = word
            target[b, rows, width:] = jnp.broadcast_to(scale, (GROUP, LANES))


def decode_rows(source, target):
    width = target.shape[1]

    @pl.loop(0, source.shape[0] // GROUP)
    def _(i):
        rows = pl.ds(pl.multiple_of(i * GROUP, GROUP), GROUP)
        target[rows, :] = decoded(source[rows, :width], source[rows, width:width + 1])


def transport(
    nr, nc, base, left, right, served, left_all, right_all, left_late, tail, mid, mid_right,
    left_code, left_codes, right_code, right_codes, *scratch,
):
    (a_send, a_recv, b_send, b_recv, fa_send, fa_recv, fb_send, fb_recv, ra_send, ra_recv, rb_send, rb_recv,
     l1_send, l1_recv, l2_send, l2_recv, l3_send, l3_recv, t_send, t_recv, own_sem, code_sem,
     left_in, left_out, right_in, right_out, left_words, left_values, right_words, right_values) = scratch
    ng = nr // nc
    planes = nr // 2
    near = planes // 2
    height = base.shape[0]
    width = base.shape[1] // nr
    depth = right.shape[0]
    rank = left.shape[0]
    left_width = left_code.shape[2]
    step = height // PARTS
    late_rows = height // LATE * LATE_PARTS
    main_rows = height - late_rows
    over_rows = main_rows - CHUNKS * step
    r = lax.axis_index("row")
    c = lax.axis_index("col")
    sibling = r + 1 - 2 * lax.rem(r, 2)

    def remote(src, dst, send, recv, row, col):
        return pltpu.make_async_remote_copy(
            src_ref=src, dst_ref=dst, send_sem=send, recv_sem=recv, device_id=(row, col), device_id_type=MESH
        )

    def shifted(value, by, size):
        return lax.rem(value + by + size, size)

    def piece(src, at, b):
        if len(src.shape) == 3:
            return src.at[b]
        return src.at[at, pl.ds(pl.multiple_of(b * width, 128), width)]

    def tall(src):
        return src.shape[-2]

    def across(k, dj, g, src, final, middle, rows, off, send, recv, act):
        j = shifted(c, dj, nc)
        here = c * ng + g == r
        at = pl.ds(pl.multiple_of(off + k * rows, 8), rows)
        source = piece(src, at, g * nc + j)
        sem = (k, dj - 1, g)

        @pl.when(here)
        def _():
            to = final.at[pl.ds(pl.multiple_of(r * tall(src) + off + k * rows, 8), rows), :]
            act(remote(source, to, send.at[sem], recv.at[sem], r, j))

        @pl.when(jnp.logical_not(here))
        def _():
            to = middle.at[c, g, at, :]
            act(remote(source, to, send.at[sem], recv.at[sem], r, j))

    def start(copy):
        copy.start()

    def wait_send(copy):
        copy.wait_send()

    def arrived(k, ds, g, src, final, middle, rows, off, send, recv):
        at = pl.ds(pl.multiple_of(off + k * rows, 8), rows)
        s = shifted(c, -ds, nc)
        here = s * ng + g == r
        sem = (k, ds - 1, g)

        @pl.when(here)
        def _():
            to = final.at[pl.ds(pl.multiple_of(r * tall(src) + off + k * rows, 8), rows), :]
            remote(to, to, send.at[sem], recv.at[sem], r, s).wait_recv()

        @pl.when(jnp.logical_not(here))
        def _():
            to = middle.at[s, g, at, :]
            remote(to, to, send.at[sem], recv.at[sem], r, s).wait_recv()

    def along(k, ds, g, src, final, middle, rows, off, send, recv, own, act, act_own):
        at = pl.ds(pl.multiple_of(off + k * rows, 8), rows)
        s = shifted(c, -ds, nc)
        to_row = s * ng + g
        if ds == 0:
            source = piece(src, at, g * nc + c)
        else:
            source = middle.at[s, g, at, :]
        to = final.at[pl.ds(pl.multiple_of(r * tall(src) + off + k * rows, 8), rows), :]

        @pl.when(to_row != r)
        def _():
            act(remote(source, to, send.at[k, ds, g], recv.at[k, r], to_row, c))

        if ds == 0:
            @pl.when(to_row == r)
            def _():
                act_own(pltpu.make_async_copy(source, to, own.at[k]))

    def received(k, dq, final, rows, off, total, send, recv):
        q = shifted(r, -dq, nr)
        to = final.at[pl.ds(pl.multiple_of(q * total + off + k * rows, 8), rows), :]
        remote(to, to, send.at[k, 0, 0], recv.at[k, q], q, c).wait_recv()

    big = (base, served, mid, step, over_rows)
    fine = (base, served, mid, (step + over_rows) // FINE, 0)
    small = (right_code, right_codes, mid_right, depth, 0)
    order = (nc // 2, *(d for d in range(1, nc) if d != nc // 2))
    own_big = own_sem.at[pl.ds(0, CHUNKS)]
    own_small = own_sem.at[pl.ds(CHUNKS, 1)]
    own_fine = own_sem.at[pl.ds(CHUNKS + 2 + ng, FINE)]

    def each_across(k, arrays, send, recv, act):
        for dj in order:
            for g in range(ng):
                across(k, dj, g, *arrays, send, recv, act)

    def each_along(k, shifts, arrays, send, recv, own, act, act_own):
        for ds in shifts:
            for g in range(ng):
                along(k, ds, g, *arrays, send, recv, own, act, act_own)

    def late_across(dj, g, act):
        j = shifted(c, dj, nc)
        source = base.at[pl.ds(main_rows, late_rows), pl.ds(pl.multiple_of((g * nc + j) * width, 128), width)]
        act(remote(source, tail.at[c * ng + g], t_send.at[dj - 1, g], t_recv.at[dj - 1, g], r, j))

    def late_arrived(ds, g):
        s = shifted(c, -ds, nc)
        to = tail.at[s * ng + g]
        remote(to, to, t_send.at[ds - 1, g], t_recv.at[ds - 1, g], r, s).wait_recv()

    def late_own(g):
        source = base.at[pl.ds(main_rows, late_rows), pl.ds(pl.multiple_of((g * nc + c) * width, 128), width)]
        return pltpu.make_async_copy(source, tail.at[c * ng + g], own_sem.at[CHUNKS + 2 + g])

    def each_late(act):
        for dj in range(1, nc):
            for g in range(ng):
                late_across(dj, g, act)

    def block(s, q):
        return left_codes.at[
            pl.ds(pl.multiple_of(s * rank, 8), rank), pl.ds(pl.multiple_of(q * left_width, 128), left_width)
        ]

    place = r // 2
    core = lax.rem(r, 2)
    first = place // near * near

    def beside(e):
        return first + lax.rem(place - first + e + near, near)

    def over(p):
        return shifted(p, near, planes)

    def held(m):
        p = beside(-(m % near))
        return (p if m < near else over(p)) * 2 + core

    def first_left(m):
        to = beside(m) if m < near else over(place)
        return remote(left_code.at[0], block(c, r), l1_send.at[m - 1], l1_recv.at[m - 1], to * 2 + core, c)

    def passed_left(m):
        q = held(near)
        return remote(block(c, q), block(c, q), l1_send.at[near + m - 1], l1_recv.at[near + m - 1], beside(m) * 2 + core, c)

    def second_left(d, dj):
        q = held(d)
        source = left_code.at[0] if d == 0 else block(c, q)
        return remote(source, block(c, q), l2_send.at[d, dj - 1], l2_recv.at[d, dj - 1], r, shifted(c, dj, nc))

    def third_left(d, ds):
        q = held(d)
        s = shifted(c, -ds, nc)
        source = left_code.at[0] if d == 0 and ds == 0 else block(s, q)
        return remote(source, block(s, q), l3_send.at[d, ds], l3_recv.at[d, ds], sibling, c)

    def got(sems_send, sems_recv, s, q):
        remote(block(s, q), block(s, q), sems_send, sems_recv, r, shifted(c, 1, nc)).wait_recv()

    def pass_left():
        got(l1_send.at[near - 1], l1_recv.at[near - 1], c, held(near))
        for m in range(1, near):
            passed_left(m).start()

    def spread_left():
        for d in range(planes):
            if d > 0 and d != near:
                got(l1_send.at[d - 1], l1_recv.at[d - 1], c, held(d))
            for dj in range(1, nc):
                second_left(d, dj).start()
            third_left(d, 0).start()

    def share_left():
        for d in range(planes):
            for ds in range(1, nc):
                got(l2_send.at[d, ds - 1], l2_recv.at[d, ds - 1], shifted(c, -ds, nc), held(d))
                third_left(d, ds).start()

    barrier = pltpu.get_barrier_semaphore()
    for dj in range(1, nc):
        pl.semaphore_signal(barrier, inc=1, device_id=(r, shifted(c, dj, nc)), device_id_type=MESH)
    for dq in range(1, nr):
        pl.semaphore_signal(barrier, inc=1, device_id=(shifted(r, dq, nr), c), device_id_type=MESH)
    pl.semaphore_wait(barrier, nc + nr - 2)

    fetch_left = pltpu.make_async_copy(left, left_in, code_sem.at[0])
    fetch_right = pltpu.make_async_copy(right, right_in, code_sem.at[1])
    fetch_left.start()
    fetch_right.start()
    for k in range(FINE):
        each_across(k, fine, fa_send, fa_recv, start)
        each_along(k, (0,), fine, fb_send, fb_recv, own_fine, start, start)

    @pl.loop(1, AHEAD + 1)
    def _(k):
        each_across(k, big, a_send, a_recv, start)

    own_left = pltpu.make_async_copy(left_code.at[0], block(c, r), own_sem.at[CHUNKS + 1])

    def send_left():
        fetch_left.wait()
        encode_rows(left_in, left_out, left.shape[1])
        keep_left = pltpu.make_async_copy(left_out, left_code, code_sem.at[2])
        keep_left.start()
        keep_left.wait()
        for m in range(near, 0, -1):
            first_left(m).start()
        own_left.start()

    def send_right():
        fetch_right.wait()
        encode_rows(right_in, right_out, width)
        keep_right = pltpu.make_async_copy(right_out, right_code, code_sem.at[3])
        keep_right.start()
        keep_right.wait()
        each_across(0, small, ra_send, ra_recv, start)
        each_along(0, (0,), small, rb_send, rb_recv, own_small, start, start)

    def forward(k, arrays, a_s, a_r, b_s, b_r, own):
        for ds in order:
            for g in range(ng):
                arrived(k, ds, g, *arrays, a_s, a_r)
                along(k, ds, g, *arrays, b_s, b_r, own, start, start)

    send_left()
    for k in range(FINE):
        forward(k, fine, fa_send, fa_recv, fb_send, fb_recv, own_fine)
    each_along(1, (0,), big, b_send, b_recv, own_big, start, start)

    @pl.loop(1, CHUNKS)
    def _(k):
        @pl.when(k + AHEAD < CHUNKS)
        def _():
            each_across(k + AHEAD, big, a_send, a_recv, start)

        @pl.when(k + AHEAD == CHUNKS)
        def _():
            each_late(start)
            for g in range(ng):
                late_own(g).start()

        forward(k, big, a_send, a_recv, b_send, b_recv, own_big)

        @pl.when(k + 1 < CHUNKS)
        def _():
            each_along(k + 1, (0,), big, b_send, b_recv, own_big, start, start)

        for at, act in ((CODE_AT, send_right), (PASS_AT, pass_left), (SPREAD_AT, spread_left), (SHARE_AT, share_left)):
            pl.when(k == at)(act)

        @pl.when(k == SMALL_AT)
        def _():
            for g in range(ng):
                for ds in order:
                    arrived(0, ds, g, *small, ra_send, ra_recv)
            each_along(0, range(1, nc), small, rb_send, rb_recv, own_small, start, start)

    for d in range(planes):
        for ds in range(nc):
            got(l3_send.at[d, ds], l3_recv.at[d, ds], shifted(c, -ds, nc), held(d) + sibling - r)
            third_left(d, ds).wait_send()
        for dj in range(1, nc):
            second_left(d, dj).wait_send()
    for m in range(1, near + 1):
        first_left(m).wait_send()
    for m in range(1, near):
        passed_left(m).wait_send()
    own_left.wait()

    def finish(copy):
        copy.wait()

    def drain(k, arrays, a, b_s, b_r, own):
        each_across(k, arrays, *a, wait_send)
        each_along(k, range(nc), arrays, b_s, b_r, own, wait_send, finish)
        for dq in range(1, nr):
            received(k, dq, arrays[1], arrays[3], arrays[4], tall(arrays[0]), b_s, b_r)

    drain(0, small, (ra_send, ra_recv), rb_send, rb_recv, own_small)
    words = pltpu.make_async_copy(right_codes, right_words, code_sem.at[0])
    words.start()
    words.wait()
    decode_rows(right_words, right_values)
    values = pltpu.make_async_copy(right_values, right_all, code_sem.at[1])
    values.start()
    values.wait()

    @pl.loop(0, nr)
    def _(q):
        part = left_codes.at[:, pl.ds(pl.multiple_of(q * left_width, 128), left_width)]
        rows = left.shape[1]
        to = left_all.at[:, pl.ds(pl.multiple_of(q * rows, 128), rows)]
        words = pltpu.make_async_copy(part, left_words, code_sem.at[2])
        words.start()
        words.wait()
        decode_rows(left_words, left_values)
        values = pltpu.make_async_copy(left_values, to, code_sem.at[3])
        values.start()
        late_to = left_late.at[:, pl.ds(pl.multiple_of(q * LANES, 128), LANES)]
        late = pltpu.make_async_copy(left_values.at[:, pl.ds(rows - LANES, LANES)], late_to, code_sem.at[2])
        late.start()
        values.wait()
        late.wait()

    each_late(wait_send)
    for g in range(ng):
        late_own(g).wait()
        for ds in range(1, nc):
            late_arrived(ds, g)
    for k in range(FINE):
        drain(k, fine, (fa_send, fa_recv), fb_send, fb_recv, own_fine)

    @pl.loop(1, CHUNKS)
    def _(k):
        drain(k, big, (a_send, a_recv), b_send, b_recv, own_big)


def move(base_weight, left_turned, right_factor):
    nr = lax.axis_size("row")
    nc = lax.axis_size("col")
    ng = nr // nc
    planes = nr // 2
    height, stored_width = base_weight.shape
    width = stored_width // nr
    depth = right_factor.shape[0]
    rank, left_width = left_turned.shape
    late_rows = height // LATE * LATE_PARTS
    main_rows = height - late_rows
    out = jax.ShapeDtypeStruct
    code = jnp.bfloat16
    vmem = pltpu.VMEM
    dma = pltpu.SemaphoreType.DMA
    anywhere = pl.BlockSpec(memory_space=pl.ANY)

    def stage_sems(chunks):
        a = (chunks, nc - 1, ng)
        return [dma(a), dma(a), dma((chunks, nc, ng)), dma((chunks, nr))]

    return pl.pallas_call(
        functools.partial(transport, nr, nc),
        out_shape=[
            out((nr * height, width), base_weight.dtype),
            out((nc * rank, nr * left_width), left_turned.dtype),
            out((nr * depth, width), right_factor.dtype),
            out((nc * rank, nr * LANES), left_turned.dtype),
            out((nr, late_rows, width), base_weight.dtype),
            out((nc, ng, main_rows, width), base_weight.dtype),
            out((nc, ng, depth, width + LANES), code),
            out((1, rank, left_width + LANES), code),
            out((nc * rank, nr * (left_width + LANES)), code),
            out((nr, depth, width + LANES), code),
            out((nr * depth, width + LANES), code),
        ],
        in_specs=[anywhere] * 3,
        out_specs=[anywhere] * 11,
        scratch_shapes=[
            *stage_sems(CHUNKS),
            *stage_sems(FINE),
            *stage_sems(1),
            dma((planes - 1,)), dma((planes - 1,)),
            dma((planes, nc - 1)), dma((planes, nc - 1)),
            dma((planes, nc)), dma((planes, nc)),
            dma((nc - 1, ng)), dma((nc - 1, ng)),
            dma((CHUNKS + 2 + ng + FINE,)), dma((4,)),
            vmem((rank, left_width), jnp.float32), vmem((1, rank, left_width + LANES), code),
            vmem((depth, stored_width), jnp.float32), vmem((nr, depth, width + LANES), code),
            vmem((nc * rank, left_width + LANES), code), vmem((nc * rank, left_width), jnp.float32),
            vmem((nr * depth, width + LANES), code), vmem((nr * depth, width), jnp.float32),
        ],
        compiler_params=pltpu.CompilerParams(collective_id=0, has_side_effects=True),
    )(base_weight, left_turned, right_factor)


def product(left, right):
    return lax.dot_general(
        left, right, (((0,), (0,)), ((), ())), precision=lax.Precision.HIGH, preferred_element_type=jnp.float32
    )


def body(base_weight, left_factor, right_factor):
    nr = lax.axis_size("row")
    height = base_weight.shape[0]
    served, left_all, right_all, left_late, tail, *_ = move(base_weight, left_factor.T, right_factor)
    late = lax.all_to_all(tail, "row", 0, 0)
    late_rows, width = late.shape[1:]
    late_delta = product(left_late, right_all).reshape(nr, -1, width)
    late_delta = lax.optimization_barrier(late_delta[:, late_delta.shape[1] - late_rows:])
    merged = (served.astype(jnp.float32) + product(left_all, right_all)).astype(jnp.bfloat16)
    late_merged = (late.astype(jnp.float32) + late_delta).astype(jnp.bfloat16)
    merged = merged.reshape(nr, height, width).at[:, height - late_rows:].set(late_merged)
    return merged.reshape(nr * height, width)


def solution(mesh):
    placed = (P("row", "col"), P("row", "col"), P("row", "col"))
    return jax.shard_map(
        body, mesh=mesh, in_specs=placed, out_specs=P(None, ("row", "col")), check_vma=False
    )
```

```python
import functools

import jax
import jax.numpy as jnp
from jax import lax
from jax.experimental import pallas as pl
from jax.experimental.pallas import tpu as pltpu
from jax.sharding import PartitionSpec as P

CHUNKS = 10
FINE = 6
LATE = 16
LATE_PARTS = 1
AHEAD = 3
CODE_AT = 3
PASS_AT = 3
SMALL_AT = 6
SPREAD_AT = 6
SHARE_AT = 9
MESH = pl.DeviceIdType.MESH
LANES = 128
GROUP = 16
OCTAVES = 251
LOWEST = -125.0
LEVELS = OCTAVES * 128.0 - 1.0


def coded(value):
    top = jnp.max(jnp.abs(value), axis=1, keepdims=True)
    scale = jnp.maximum(top * 1.01, 1e-30).astype(jnp.bfloat16)
    level = jnp.floor(jnp.abs(value) * (LEVELS / scale.astype(jnp.float32)) + 0.5)
    octave = jnp.floor(level * (1.0 / 128.0))
    word = (level * (1.0 / 128.0) - octave + 1.0) * jnp.exp2(octave + LOWEST)
    return jnp.where(value < 0.0, -word, word).astype(jnp.bfloat16), scale


def decoded(word, scale):
    word = word.astype(jnp.float32)
    size = jnp.abs(word)
    octave = jnp.floor(jnp.log2(size))
    level = jnp.floor((octave - LOWEST + (size * jnp.exp2(-octave) - 1.0)) * 128.0 + 0.5)
    value = level * (scale.astype(jnp.float32) * (1.0 / LEVELS))
    return jnp.where(word < 0.0, -value, value)


def encode_rows(source, target, width):
    @pl.loop(0, source.shape[0] // GROUP)
    def _(i):
        rows = pl.ds(pl.multiple_of(i * GROUP, GROUP), GROUP)
        for b in range(source.shape[1] // width):
            word, scale = coded(source[rows, b * width:(b + 1) * width])
            target[b, rows, :width] = word
            target[b, rows, width:] = jnp.broadcast_to(scale, (GROUP, LANES))


def decode_rows(source, target):
    width = target.shape[1]

    @pl.loop(0, source.shape[0] // GROUP)
    def _(i):
        rows = pl.ds(pl.multiple_of(i * GROUP, GROUP), GROUP)
        target[rows, :] = decoded(source[rows, :width], source[rows, width:width + 1])


def transport(
    nr, nc, base, left, right, served, left_all, right_all, left_late, tail, mid, mid_right,
    left_code, left_codes, right_code, right_codes, *scratch,
):
    (a_send, a_recv, b_send, b_recv, fa_send, fa_recv, fb_send, fb_recv, ra_send, ra_recv, rb_send, rb_recv,
     l1_send, l1_recv, l2_send, l2_recv, l3_send, l3_recv, t_send, t_recv, own_sem, code_sem,
     left_in, left_out, right_in, right_out, left_words, left_values, right_words, right_values) = scratch
    ng = nr // nc
    planes = nr // 2
    near = planes // 2
    height = base.shape[0]
    width = base.shape[1] // nr
    depth = right.shape[0]
    rank = left.shape[0]
    left_width = left_code.shape[2]
    late_rows = height // LATE * LATE_PARTS
    main_rows = height - late_rows
    step = main_rows // CHUNKS
    over_rows = main_rows - CHUNKS * step
    r = lax.axis_index("row")
    c = lax.axis_index("col")
    sibling = r + 1 - 2 * lax.rem(r, 2)

    def remote(src, dst, send, recv, row, col):
        return pltpu.make_async_remote_copy(
            src_ref=src, dst_ref=dst, send_sem=send, recv_sem=recv, device_id=(row, col), device_id_type=MESH
        )

    def shifted(value, by, size):
        return lax.rem(value + by + size, size)

    def piece(src, at, b):
        if len(src.shape) == 3:
            return src.at[b]
        return src.at[at, pl.ds(pl.multiple_of(b * width, 128), width)]

    def tall(src):
        return src.shape[-2]

    def across(k, dj, g, src, final, middle, rows, off, send, recv, act):
        j = shifted(c, dj, nc)
        here = c * ng + g == r
        at = pl.ds(pl.multiple_of(off + k * rows, 8), rows)
        source = piece(src, at, g * nc + j)
        sem = (k, dj - 1, g)

        @pl.when(here)
        def _():
            to = final.at[pl.ds(pl.multiple_of(r * tall(src) + off + k * rows, 8), rows), :]
            act(remote(source, to, send.at[sem], recv.at[sem], r, j))

        @pl.when(jnp.logical_not(here))
        def _():
            to = middle.at[c, g, at, :]
            act(remote(source, to, send.at[sem], recv.at[sem], r, j))

    def start(copy):
        copy.start()

    def wait_send(copy):
        copy.wait_send()

    def arrived(k, ds, g, src, final, middle, rows, off, send, recv):
        at = pl.ds(pl.multiple_of(off + k * rows, 8), rows)
        s = shifted(c, -ds, nc)
        here = s * ng + g == r
        sem = (k, ds - 1, g)

        @pl.when(here)
        def _():
            to = final.at[pl.ds(pl.multiple_of(r * tall(src) + off + k * rows, 8), rows), :]
            remote(to, to, send.at[sem], recv.at[sem], r, s).wait_recv()

        @pl.when(jnp.logical_not(here))
        def _():
            to = middle.at[s, g, at, :]
            remote(to, to, send.at[sem], recv.at[sem], r, s).wait_recv()

    def along(k, ds, g, src, final, middle, rows, off, send, recv, own, act, act_own):
        at = pl.ds(pl.multiple_of(off + k * rows, 8), rows)
        s = shifted(c, -ds, nc)
        to_row = s * ng + g
        if ds == 0:
            source = piece(src, at, g * nc + c)
        else:
            source = middle.at[s, g, at, :]
        to = final.at[pl.ds(pl.multiple_of(r * tall(src) + off + k * rows, 8), rows), :]

        @pl.when(to_row != r)
        def _():
            act(remote(source, to, send.at[k, ds, g], recv.at[k, r], to_row, c))

        if ds == 0:
            @pl.when(to_row == r)
            def _():
                act_own(pltpu.make_async_copy(source, to, own.at[k]))

    def received(k, dq, final, rows, off, total, send, recv):
        q = shifted(r, -dq, nr)
        to = final.at[pl.ds(pl.multiple_of(q * total + off + k * rows, 8), rows), :]
        remote(to, to, send.at[k, 0, 0], recv.at[k, q], q, c).wait_recv()

    big = (base, served, mid, step, over_rows)
    fine = (base, served, mid, (step + over_rows) // FINE, 0)
    small = (right_code, right_codes, mid_right, depth, 0)
    order = (nc // 2, *(d for d in range(1, nc) if d != nc // 2))
    own_big = own_sem.at[pl.ds(0, CHUNKS)]
    own_small = own_sem.at[pl.ds(CHUNKS, 1)]
    own_fine = own_sem.at[pl.ds(CHUNKS + 2 + ng, FINE)]

    def each_across(k, arrays, send, recv, act):
        for dj in order:
            for g in range(ng):
                across(k, dj, g, *arrays, send, recv, act)

    def each_along(k, shifts, arrays, send, recv, own, act, act_own):
        for ds in shifts:
            for g in range(ng):
                along(k, ds, g, *arrays, send, recv, own, act, act_own)

    def late_across(dj, g, act):
        j = shifted(c, dj, nc)
        source = base.at[pl.ds(main_rows, late_rows), pl.ds(pl.multiple_of((g * nc + j) * width, 128), width)]
        act(remote(source, tail.at[c * ng + g], t_send.at[dj - 1, g], t_recv.at[dj - 1, g], r, j))

    def late_arrived(ds, g):
        s = shifted(c, -ds, nc)
        to = tail.at[s * ng + g]
        remote(to, to, t_send.at[ds - 1, g], t_recv.at[ds - 1, g], r, s).wait_recv()

    def late_own(g):
        source = base.at[pl.ds(main_rows, late_rows), pl.ds(pl.multiple_of((g * nc + c) * width, 128), width)]
        return pltpu.make_async_copy(source, tail.at[c * ng + g], own_sem.at[CHUNKS + 2 + g])

    def each_late(act):
        for dj in range(1, nc):
            for g in range(ng):
                late_across(dj, g, act)

    def block(s, q):
        return left_codes.at[
            pl.ds(pl.multiple_of(s * rank, 8), rank), pl.ds(pl.multiple_of(q * left_width, 128), left_width)
        ]

    place = r // 2
    core = lax.rem(r, 2)
    first = place // near * near

    def beside(e):
        return first + lax.rem(place - first + e + near, near)

    def over(p):
        return shifted(p, near, planes)

    def held(m):
        p = beside(-(m % near))
        return (p if m < near else over(p)) * 2 + core

    def first_left(m):
        to = beside(m) if m < near else over(place)
        return remote(left_code.at[0], block(c, r), l1_send.at[m - 1], l1_recv.at[m - 1], to * 2 + core, c)

    def passed_left(m):
        q = held(near)
        return remote(block(c, q), block(c, q), l1_send.at[near + m - 1], l1_recv.at[near + m - 1], beside(m) * 2 + core, c)

    def second_left(d, dj):
        q = held(d)
        source = left_code.at[0] if d == 0 else block(c, q)
        return remote(source, block(c, q), l2_send.at[d, dj - 1], l2_recv.at[d, dj - 1], r, shifted(c, dj, nc))

    def third_left(d, ds):
        q = held(d)
        s = shifted(c, -ds, nc)
        source = left_code.at[0] if d == 0 and ds == 0 else block(s, q)
        return remote(source, block(s, q), l3_send.at[d, ds], l3_recv.at[d, ds], sibling, c)

    def got(sems_send, sems_recv, s, q):
        remote(block(s, q), block(s, q), sems_send, sems_recv, r, shifted(c, 1, nc)).wait_recv()

    def pass_left():
        got(l1_send.at[near - 1], l1_recv.at[near - 1], c, held(near))
        for m in range(1, near):
            passed_left(m).start()

    def spread_left():
        for d in range(planes):
            if d > 0 and d != near:
                got(l1_send.at[d - 1], l1_recv.at[d - 1], c, held(d))
            for dj in range(1, nc):
                second_left(d, dj).start()
            third_left(d, 0).start()

    def share_left():
        for d in range(planes):
            for ds in range(1, nc):
                got(l2_send.at[d, ds - 1], l2_recv.at[d, ds - 1], shifted(c, -ds, nc), held(d))
                third_left(d, ds).start()

    barrier = pltpu.get_barrier_semaphore()
    for dj in range(1, nc):
        pl.semaphore_signal(barrier, inc=1, device_id=(r, shifted(c, dj, nc)), device_id_type=MESH)
    for dq in range(1, nr):
        pl.semaphore_signal(barrier, inc=1, device_id=(shifted(r, dq, nr), c), device_id_type=MESH)
    pl.semaphore_wait(barrier, nc + nr - 2)

    fetch_left = pltpu.make_async_copy(left, left_in, code_sem.at[0])
    fetch_right = pltpu.make_async_copy(right, right_in, code_sem.at[1])
    fetch_left.start()
    fetch_right.start()
    for k in range(FINE):
        each_across(k, fine, fa_send, fa_recv, start)
        each_along(k, (0,), fine, fb_send, fb_recv, own_fine, start, start)

    @pl.loop(1, AHEAD + 1)
    def _(k):
        each_across(k, big, a_send, a_recv, start)

    own_left = pltpu.make_async_copy(left_code.at[0], block(c, r), own_sem.at[CHUNKS + 1])

    def send_left():
        fetch_left.wait()
        encode_rows(left_in, left_out, left.shape[1])
        keep_left = pltpu.make_async_copy(left_out, left_code, code_sem.at[2])
        keep_left.start()
        keep_left.wait()
        for m in range(near, 0, -1):
            first_left(m).start()
        own_left.start()

    def send_right():
        fetch_right.wait()
        encode_rows(right_in, right_out, width)
        keep_right = pltpu.make_async_copy(right_out, right_code, code_sem.at[3])
        keep_right.start()
        keep_right.wait()
        each_across(0, small, ra_send, ra_recv, start)
        each_along(0, (0,), small, rb_send, rb_recv, own_small, start, start)

    def forward(k, arrays, a_s, a_r, b_s, b_r, own):
        for ds in order:
            for g in range(ng):
                arrived(k, ds, g, *arrays, a_s, a_r)
                along(k, ds, g, *arrays, b_s, b_r, own, start, start)

    send_left()
    for k in range(FINE):
        forward(k, fine, fa_send, fa_recv, fb_send, fb_recv, own_fine)
    each_along(1, (0,), big, b_send, b_recv, own_big, start, start)

    @pl.loop(1, CHUNKS)
    def _(k):
        @pl.when(k + AHEAD < CHUNKS)
        def _():
            each_across(k + AHEAD, big, a_send, a_recv, start)

        @pl.when(k + AHEAD == CHUNKS)
        def _():
            each_late(start)
            for g in range(ng):
                late_own(g).start()

        forward(k, big, a_send, a_recv, b_send, b_recv, own_big)

        @pl.when(k + 1 < CHUNKS)
        def _():
            each_along(k + 1, (0,), big, b_send, b_recv, own_big, start, start)

        for at, act in ((CODE_AT, send_right), (PASS_AT, pass_left), (SPREAD_AT, spread_left), (SHARE_AT, share_left)):
            pl.when(k == at)(act)

        @pl.when(k == SMALL_AT)
        def _():
            for g in range(ng):
                for ds in order:
                    arrived(0, ds, g, *small, ra_send, ra_recv)
            each_along(0, range(1, nc), small, rb_send, rb_recv, own_small, start, start)

    for d in range(planes):
        for ds in range(nc):
            got(l3_send.at[d, ds], l3_recv.at[d, ds], shifted(c, -ds, nc), held(d) + sibling - r)
            third_left(d, ds).wait_send()
        for dj in range(1, nc):
            second_left(d, dj).wait_send()
    for m in range(1, near + 1):
        first_left(m).wait_send()
    for m in range(1, near):
        passed_left(m).wait_send()
    own_left.wait()

    def finish(copy):
        copy.wait()

    def drain(k, arrays, a, b_s, b_r, own):
        each_across(k, arrays, *a, wait_send)
        each_along(k, range(nc), arrays, b_s, b_r, own, wait_send, finish)
        for dq in range(1, nr):
            received(k, dq, arrays[1], arrays[3], arrays[4], tall(arrays[0]), b_s, b_r)

    drain(0, small, (ra_send, ra_recv), rb_send, rb_recv, own_small)
    words = pltpu.make_async_copy(right_codes, right_words, code_sem.at[0])
    words.start()
    words.wait()
    decode_rows(right_words, right_values)
    values = pltpu.make_async_copy(right_values, right_all, code_sem.at[1])
    values.start()
    values.wait()

    @pl.loop(0, nr)
    def _(q):
        part = left_codes.at[:, pl.ds(pl.multiple_of(q * left_width, 128), left_width)]
        rows = left.shape[1]
        to = left_all.at[:, pl.ds(pl.multiple_of(q * rows, 128), rows)]
        words = pltpu.make_async_copy(part, left_words, code_sem.at[2])
        words.start()
        words.wait()
        decode_rows(left_words, left_values)
        values = pltpu.make_async_copy(left_values, to, code_sem.at[3])
        values.start()
        late_to = left_late.at[:, pl.ds(pl.multiple_of(q * LANES, 128), LANES)]
        late = pltpu.make_async_copy(left_values.at[:, pl.ds(rows - LANES, LANES)], late_to, code_sem.at[2])
        late.start()
        values.wait()
        late.wait()

    each_late(wait_send)
    for g in range(ng):
        late_own(g).wait()
        for ds in range(1, nc):
            late_arrived(ds, g)
    for k in range(FINE):
        drain(k, fine, (fa_send, fa_recv), fb_send, fb_recv, own_fine)

    @pl.loop(1, CHUNKS)
    def _(k):
        drain(k, big, (a_send, a_recv), b_send, b_recv, own_big)


def move(base_weight, left_turned, right_factor):
    nr = lax.axis_size("row")
    nc = lax.axis_size("col")
    ng = nr // nc
    planes = nr // 2
    height, stored_width = base_weight.shape
    width = stored_width // nr
    depth = right_factor.shape[0]
    rank, left_width = left_turned.shape
    late_rows = height // LATE * LATE_PARTS
    main_rows = height - late_rows
    out = jax.ShapeDtypeStruct
    code = jnp.bfloat16
    vmem = pltpu.VMEM
    dma = pltpu.SemaphoreType.DMA
    anywhere = pl.BlockSpec(memory_space=pl.ANY)

    def stage_sems(chunks):
        a = (chunks, nc - 1, ng)
        return [dma(a), dma(a), dma((chunks, nc, ng)), dma((chunks, nr))]

    return pl.pallas_call(
        functools.partial(transport, nr, nc),
        out_shape=[
            out((nr * height, width), base_weight.dtype),
            out((nc * rank, nr * left_width), left_turned.dtype),
            out((nr * depth, width), right_factor.dtype),
            out((nc * rank, nr * LANES), left_turned.dtype),
            out((nr, late_rows, width), base_weight.dtype),
            out((nc, ng, main_rows, width), base_weight.dtype),
            out((nc, ng, depth, width + LANES), code),
            out((1, rank, left_width + LANES), code),
            out((nc * rank, nr * (left_width + LANES)), code),
            out((nr, depth, width + LANES), code),
            out((nr * depth, width + LANES), code),
        ],
        in_specs=[anywhere] * 3,
        out_specs=[anywhere] * 11,
        scratch_shapes=[
            *stage_sems(CHUNKS),
            *stage_sems(FINE),
            *stage_sems(1),
            dma((planes - 1,)), dma((planes - 1,)),
            dma((planes, nc - 1)), dma((planes, nc - 1)),
            dma((planes, nc)), dma((planes, nc)),
            dma((nc - 1, ng)), dma((nc - 1, ng)),
            dma((CHUNKS + 2 + ng + FINE,)), dma((4,)),
            vmem((rank, left_width), jnp.float32), vmem((1, rank, left_width + LANES), code),
            vmem((depth, stored_width), jnp.float32), vmem((nr, depth, width + LANES), code),
            vmem((nc * rank, left_width + LANES), code), vmem((nc * rank, left_width), jnp.float32),
            vmem((nr * depth, width + LANES), code), vmem((nr * depth, width), jnp.float32),
        ],
        compiler_params=pltpu.CompilerParams(collective_id=0, has_side_effects=True),
    )(base_weight, left_turned, right_factor)


def product(left, right):
    return lax.dot_general(
        left, right, (((0,), (0,)), ((), ())), precision=lax.Precision.HIGH, preferred_element_type=jnp.float32
    )


def body(base_weight, left_factor, right_factor):
    nr = lax.axis_size("row")
    height = base_weight.shape[0]
    served, left_all, right_all, left_late, tail, *_ = move(base_weight, left_factor.T, right_factor)
    late = lax.all_to_all(tail, "row", 0, 0)
    late_rows, width = late.shape[1:]
    late_delta = product(left_late, right_all).reshape(nr, -1, width)
    late_delta = lax.optimization_barrier(late_delta[:, late_delta.shape[1] - late_rows:])
    merged = (served.astype(jnp.float32) + product(left_all, right_all)).astype(jnp.bfloat16)
    late_merged = (late.astype(jnp.float32) + late_delta).astype(jnp.bfloat16)
    merged = merged.reshape(nr, height, width).at[:, height - late_rows:].set(late_merged)
    return merged.reshape(nr * height, width)


def solution(mesh):
    placed = (P("row", "col"), P("row", "col"), P("row", "col"))
    return jax.shard_map(
        body, mesh=mesh, in_specs=placed, out_specs=P(None, ("row", "col")), check_vma=False
    )
```
